32 devices in a mesh: frame: 8 (over y, x, core), expert: 4 (over z).
Axes of the slice: x: 2, y: 2, z: 4, core: 2. Of those that a mesh axis runs over, the one named last changes fastest.
Arguments:
- patches: bfloat16 [8, 4, 256, 1536], P('frame', 'expert'), may hold values from -6 to 6
- temporal_q: bfloat16 [8, 4, 256, 1536], P('frame', 'expert'), may hold values from -70 to 70
- temporal_k: bfloat16 [8, 4, 256, 1536], P('frame', 'expert'), may hold values from -6 to 6
- temporal_v: bfloat16 [8, 4, 256, 1536], P('frame', 'expert'), may hold values from -6 to 6
- clip_lengths: int32 [4], P('expert'), may hold values from 1 to 8
- w_time: bfloat16 [1536, 1536], replicated, may hold values from -0.15625 to 0.15625
- gain_space: float32 [1536], replicated, may hold values from 0.1 to 1.9
- w_space: bfloat16 [1536, 4608], P(None, 'frame'), may hold values from -2 to 2
- w_merge: bfloat16 [1536, 1536], replicated, may hold values from -0.15625 to 0.15625
- gain_mix: float32 [1536], replicated, may hold values from 0.1 to 1.9
- expert_ids: int32 [8, 4, 256, 2], P('frame', 'expert'), may hold values from 0 to 31, all different within a row; in each aligned block of 256 rows (0 to 255, 256 to 511, ..., all dimensions but the last counted through in order) at most 18 rows name the same one
- gate_weights: float32 [8, 4, 256, 2], P('frame', 'expert'), may hold values from 0.25 to 1
- w_expand: bfloat16 [32, 1536, 6144], P(('frame', 'expert')), may hold values from -0.15625 to 0.15625
- w_reduce: bfloat16 [32, 6144, 1536], P(('frame', 'expert')), may hold values from -0.078125 to 0.078125
Outputs:
- block_out: bfloat16 [8, 4, 256, 1536], P('frame', 'expert')
The draws below stay inside these ranges and needn't reach their ends.
Inputs may be any that keep to these rules, and one draw needn't show every extreme that they name: `expert_ids`: the rows of one device (the 256 rows of one frame and 1 clips) name no expert more than 18 times, and in some device's rows an expert is named exactly 18 times; the two experts of a row differ.
All inputs are finite; a program needn't handle non-finite values.
Results may differ from the reference program's by a relative error of at most 0.0065.
Values may be sent and summed in bfloat16 or wider, within the bound.
A program may use at most 128 MiB of HBM per device.

```python
import math
import jax
import jax.numpy as jnp
import numpy as np
from jax import lax

D = 1536
HEADS = 24
FF_EXPERT = 6144
EXPERTS = 32
PATCHES = 256
FRAMES = 8
CLIPS = 4
ROWS_DEV = 256
CAP = 18
SHARDS = 1
HID_DEV = 6144
DEVICES = 32


def query_key_pair(key):
    full_shape = (FRAMES, CLIPS, PATCHES, D)
    key_rows = jnp.clip(jax.random.normal(jax.random.fold_in(key, 11), full_shape, jnp.float32), -6.0, 6.0)
    queries = jnp.clip(jax.random.normal(jax.random.fold_in(key, 12), full_shape, jnp.float32), -6.0, 6.0)
    return (queries, key_rows)


def draw_temporal_q(key, part):
    return query_key_pair(key)[0].astype(jnp.bfloat16)


def draw_temporal_k(key, part):
    return query_key_pair(key)[1].astype(jnp.bfloat16)


def draw_w_space(key, part):
    factor = D ** (-0.5)
    base = jax.random.normal(jax.random.fold_in(key, 21), (D, 3 * D), jnp.float32) * factor
    return base.astype(jnp.bfloat16)


def plant(array, stream_key, low, largest):
    index_at = [jax.random.randint(jax.random.fold_in(stream_key, axis), (), 0, length) for axis, length in enumerate(array.shape)]
    main_axis = array.shape.index(max(array.shape))
    beside = index_at[:main_axis] + [(index_at[main_axis] + 1) % array.shape[main_axis]] + index_at[main_axis + 1:]
    return array.at[tuple(index_at)].set(low).at[tuple(beside)].set(largest)


def block_scale(stream_key, extent, shards, smallest, largest):
    factor_of, own = 1.0, jax.random.fold_in(stream_key, 6)
    for axis_at, shards_of in shards:
        draws = jnp.exp(jax.random.uniform(jax.random.fold_in(own, axis_at), (shards_of,), jnp.float32, smallest / len(shards), largest / len(shards)))
        factor_of = factor_of * jnp.repeat(draws, extent[axis_at] // shards_of).reshape([-1 if axis == axis_at else 1 for axis in range(len(extent))])
    return factor_of


def routed_block(own_key, own, number, rows, amount, top, most, skew):
    ranking = jax.random.permutation(own_key, amount)
    crowded, usual = portions_of(amount, rows * top, most, skew, True), portions_of(amount, rows * top, most, skew, False)
    places = jnp.arange(amount)

    def named(lengths, rotation):
        used = int((lengths > 0).sum())
        fixed = max(1, used // 4)
        shifted = fixed + (places - fixed + rotation * (used - fixed)) % max(1, amount - fixed)
        return jnp.zeros((amount,), jnp.int32).at[ranking[jnp.where(places < fixed, places, shifted)]].set(jnp.asarray(lengths, jnp.int32))

    lengths = jnp.where(number % 4 == 0, named(crowded, number // 4), named(usual, number - number // 4 - 1))
    mixed = jax.random.permutation(jax.random.fold_in(own, 3), amount)
    giver, sink = mixed[0:amount // 2 * 2:2], mixed[1:amount // 2 * 2:2]
    room = jnp.minimum(lengths[giver] - 1, most - lengths[sink]) // 2
    room = jnp.where((giver == ranking[0]) | (sink == ranking[0]) | (lengths[sink] == 0), 0, jnp.maximum(room, 0))
    shifted = jax.random.randint(jax.random.fold_in(own, 4), (amount // 2,), 0, 1 << 20) % (room + 1)
    lengths = lengths.at[giver].add(-shifted).at[sink].add(shifted)
    labels = jnp.searchsorted(jnp.cumsum(lengths), jnp.arange(rows * top), side="right").astype(jnp.int32)
    grid = labels.reshape(top, rows).T
    grid = grid[jax.random.permutation(jax.random.fold_in(own, 1), rows)]
    rotation = jax.random.randint(jax.random.fold_in(own, 2), (rows, 1), 0, top)
    return jnp.take_along_axis(grid, (jnp.arange(top)[None, :] + rotation) % top, axis=1)


def portions_of(number_of, total, reach, skew, full):
    portions = [(1 << 20) // math.isqrt(standing ** skew) + 1 for standing in range(1, number_of + 1)]
    largest = reach if full else min(reach, max(-(-total // number_of), total * portions[0] // sum(portions)))
    least = 1 if total - largest >= number_of - 1 else 0
    given, surplus = [largest] + [least] * (number_of - 1), total - largest - least * (number_of - 1)
    while surplus > 0:
        movable = [i for i in range(1, number_of) if given[i] < largest] or [i for i in range(1, number_of) if given[i] < reach]
        mass, budget = sum([portions[i] for i in movable]), surplus
        for i in movable:
            addition = min(reach - given[i], max(1, budget * portions[i] // mass), surplus)
            given[i] = given[i] + addition
            surplus = surplus - addition
    return np.array(given)


def scatter_about(rng, dims, deviation, limit, pieces=(), kind=jnp.bfloat16):
    factor_of = block_scale(rng, dims, pieces, -0.22, 0.18) if pieces else 1.0
    array = jax.random.normal(rng, dims, jnp.float32) * deviation * factor_of
    return jnp.minimum(jnp.maximum(array, -limit), limit).astype(kind)


def setup_inputs(seed: int = 0) -> dict:
    keys = jax.random.split(jax.random.key(seed), 15)
    patches = scatter_about(keys[0], (FRAMES, CLIPS, PATCHES, D), 1.0, 6.0, ((0, 8), (1, 4)))
    temporal_q = draw_temporal_q(jax.random.fold_in(keys[14], 71), 0)
    temporal_k = draw_temporal_k(jax.random.fold_in(keys[14], 71), 0)
    temporal_v = scatter_about(keys[3], (FRAMES, CLIPS, PATCHES, D), 1.0, 6.0, ((0, 8), (1, 4)))
    clip_lengths = plant(jax.random.randint(keys[4], (CLIPS,), 1, FRAMES + 1), jax.random.fold_in(keys[4], 1), 1, FRAMES).astype(jnp.int32)
    w_time = scatter_about(keys[5], (D, D), D ** -0.5, 0.15625)
    gain_space = jnp.clip(1.0 + 0.18 * jax.random.normal(keys[6], (D,), jnp.float32), 0.1, 1.9)
    w_space = draw_w_space(jax.random.fold_in(keys[14], 71), 0)
    w_merge = scatter_about(keys[8], (D, D), D ** -0.5, 0.15625)
    gain_mix = jnp.clip(1.0 + 0.18 * jax.random.normal(keys[9], (D,), jnp.float32), 0.1, 1.9)
    expert_ids_keys = jax.random.split(jax.random.fold_in(keys[10], 1), FRAMES * CLIPS * PATCHES // ROWS_DEV)
    expert_ids_turns = jax.random.permutation(jax.random.fold_in(keys[10], 3), FRAMES * CLIPS * PATCHES // ROWS_DEV)
    expert_ids = jax.vmap(lambda own, number: routed_block(jax.random.fold_in(keys[10], 2), own, number, ROWS_DEV, EXPERTS, 2, CAP, 2))(expert_ids_keys, expert_ids_turns).reshape((FRAMES, CLIPS, PATCHES, 2))
    gate_weights = jnp.clip(0.25 + 0.75 * jax.random.uniform(keys[11], (FRAMES, CLIPS, PATCHES, 2), jnp.float32) ** block_scale(keys[11], (FRAMES, CLIPS, PATCHES, 2), ((0, 8), (1, 4)), -0.2, 0.2), 0.25, 1.0)
    w_expand = scatter_about(keys[12], (DEVICES, D, HID_DEV), D ** -0.5, 0.15625, ((0, 32),))
    w_reduce = scatter_about(keys[13], (DEVICES, HID_DEV, D), FF_EXPERT ** -0.5, 0.078125, ((0, 32),))
    return dict(patches=patches, temporal_q=temporal_q, temporal_k=temporal_k, temporal_v=temporal_v, clip_lengths=clip_lengths, w_time=w_time, gain_space=gain_space, w_space=w_space, w_merge=w_merge, gain_mix=gain_mix, expert_ids=expert_ids, gate_weights=gate_weights, w_expand=w_expand, w_reduce=w_reduce)


epsilon = 1e-06

def layer_norm(values, gain_vector):
    centre = values - lax.optimization_barrier(jnp.mean(values, axis=-1, keepdims=True))
    spread = lax.optimization_barrier(jnp.mean(centre * centre, axis=-1, keepdims=True))
    return (centre * lax.rsqrt(spread + epsilon) * gain_vector.astype(jnp.float32)).astype(jnp.bfloat16)

def softmax_rows(scores):
    top_score = lax.optimization_barrier(jnp.max(scores, axis=-1, keepdims=True))
    powers = jnp.exp(scores - top_score)
    return (powers / lax.optimization_barrier(jnp.sum(powers, axis=-1, keepdims=True))).astype(jnp.bfloat16)

def time_attention(queries, key_rows, value_rows, clip_lengths):
    frame_count, clip_count, place_count, model_width = queries.shape
    head_size = model_width // HEADS

    def split_heads(array_in):
        return array_in.astype(jnp.float32).reshape(frame_count, clip_count, place_count, HEADS, head_size)
    scores = jnp.einsum('fcphd,gcphd->cphfg', split_heads(queries), split_heads(key_rows)) / math.sqrt(head_size)
    valid_keys = jnp.arange(frame_count, dtype=jnp.int32)[None, :] < clip_lengths[:, None]
    scores = jnp.where(valid_keys[:, None, None, None, :], scores, -1e+30)
    weights = softmax_rows(scores)
    attended = jnp.einsum('cphfg,gcphd->fcphd', weights.astype(jnp.float32), split_heads(value_rows))
    return attended.astype(jnp.bfloat16).reshape(frame_count, clip_count, place_count, model_width)

def space_attention(projected):
    clip_count, place_count, triple = projected.shape
    model_width = triple // 3
    head_size = model_width // HEADS
    split_parts = projected.astype(jnp.float32).reshape(clip_count, place_count, 3, HEADS, head_size)
    scores = jnp.einsum('cphd,cqhd->chpq', split_parts[:, :, 0], split_parts[:, :, 1]) / math.sqrt(head_size)
    weights = softmax_rows(scores)
    attended = jnp.einsum('chpq,cqhd->cphd', weights.astype(jnp.float32), split_parts[:, :, 2])
    return attended.astype(jnp.bfloat16).reshape(clip_count, place_count, model_width)

def expert_slots(routes):
    onehot = (routes[..., None] == jnp.arange(EXPERTS, dtype=jnp.int32)).astype(jnp.int32)
    earlier = jnp.cumsum(onehot, axis=-2) - onehot
    return lax.optimization_barrier(jnp.sum(earlier * onehot, axis=-1)).astype(jnp.int32)

def reference(patches, temporal_q, temporal_k, temporal_v, clip_lengths, w_time, gain_space, w_space, w_merge, gain_mix, expert_ids, gate_weights, w_expand, w_reduce):
    model_width = D
    full_shape = patches.shape
    time_mixed = time_attention(temporal_q, temporal_k, temporal_v, clip_lengths)
    after_time = patches.astype(jnp.float32) + jnp.dot(time_mixed.reshape(-1, model_width), w_time, preferred_element_type=jnp.float32).reshape(full_shape)
    normed = layer_norm(after_time, gain_space).reshape(-1, model_width)
    projected = jnp.dot(normed, w_space, preferred_element_type=jnp.float32).astype(jnp.bfloat16)
    projected = projected.reshape(FRAMES, CLIPS, PATCHES, 3 * model_width)
    spatial = lax.map(space_attention, projected)
    after_space = after_time + jnp.dot(spatial.reshape(-1, model_width), w_merge, preferred_element_type=jnp.float32).reshape(full_shape)
    mixed_in = layer_norm(after_space, gain_mix).reshape(DEVICES, ROWS_DEV, model_width)
    routes = expert_ids.reshape(DEVICES, ROWS_DEV * 2).astype(jnp.int32)
    slot_index = expert_slots(routes)
    owner_index = jnp.arange(DEVICES, dtype=jnp.int32)[:, None]
    position = ((routes * DEVICES + owner_index) * CAP + slot_index).reshape(-1).astype(jnp.int32)
    sources = jnp.repeat(mixed_in, 2, axis=1).reshape(-1, model_width)
    buffer_rows = jnp.zeros((EXPERTS * DEVICES * CAP, model_width), jnp.bfloat16).at[position].set(sources)
    expand = w_expand.reshape(EXPERTS, SHARDS, model_width, HID_DEV)
    reduce_part = w_reduce.reshape(EXPERTS, SHARDS, HID_DEV, model_width)

    def run_expert(operands):
        token_rows, expand_blocks, reduce_blocks = operands
        running_sum = jnp.zeros((token_rows.shape[0], model_width), jnp.float32)
        for shard_index in range(SHARDS):
            hidden = jax.nn.gelu(jnp.dot(token_rows, expand_blocks[shard_index], preferred_element_type=jnp.float32), approximate=False).astype(jnp.bfloat16)
            partial_rows = jnp.dot(hidden, reduce_blocks[shard_index], preferred_element_type=jnp.float32).astype(jnp.bfloat16)
            running_sum = running_sum + lax.optimization_barrier(partial_rows).astype(jnp.float32)
        return running_sum
    results = lax.map(run_expert, (buffer_rows.reshape(EXPERTS, DEVICES * CAP, model_width), expand, reduce_part))
    picked = results.reshape(-1, model_width)[position].reshape(DEVICES, ROWS_DEV, 2, model_width)
    gate_rows = gate_weights.reshape(DEVICES, ROWS_DEV, 2, 1)
    expert_mix = picked[:, :, 0] * gate_rows[:, :, 0] + picked[:, :, 1] * gate_rows[:, :, 1]
    return (after_space + expert_mix.reshape(full_shape)).astype(jnp.bfloat16)
```

```python
import functools
import math

import jax
import jax.numpy as jnp
from jax import lax
from jax.experimental import pallas as pl
from jax.experimental.pallas import tpu as pltpu
from jax.sharding import PartitionSpec as P

HEADS = 24
EXPERTS = 32
CAP = 18


epsilon = 1e-06


def layer_norm(values, gain_vector):
    centre = values - jnp.mean(values, axis=-1, keepdims=True)
    spread = jnp.mean(centre * centre, axis=-1, keepdims=True)
    return (centre * lax.rsqrt(spread + epsilon) * gain_vector).astype(jnp.bfloat16)


def softmax_rows(scores):
    top_score = jnp.max(scores, axis=-1, keepdims=True)
    powers = jnp.exp(scores - top_score)
    return (powers / jnp.sum(powers, axis=-1, keepdims=True)).astype(jnp.bfloat16)


def time_kernel(head_size, length_ref, q_ref, k_ref, v_ref, fold_ref, spread_ref, out_ref):
    frame_count, row_count, model_width = k_ref.shape
    lanes = fold_ref.shape[1]
    fold = fold_ref[...]
    spread = spread_ref[...]
    valid = (
        lax.broadcasted_iota(jnp.int32, (frame_count, row_count, lanes), 0) < length_ref[0]
    )

    def one_frame(frame, carry):
        product = q_ref[frame].astype(jnp.float32)[None] * k_ref[...].astype(jnp.float32)
        product = product.reshape(frame_count * row_count, model_width)
        upper = product.astype(jnp.bfloat16)
        lower = (product - upper.astype(jnp.float32)).astype(jnp.bfloat16)
        scores = jnp.dot(upper, fold, preferred_element_type=jnp.float32) + jnp.dot(
            lower, fold, preferred_element_type=jnp.float32
        )
        scores = scores.reshape(frame_count, row_count, lanes) / math.sqrt(head_size)
        scores = jnp.where(valid, scores, -1e30)
        powers = jnp.exp(scores - jnp.max(scores, axis=0, keepdims=True))
        weights = (powers / jnp.sum(powers, axis=0, keepdims=True)).astype(jnp.bfloat16)
        wide = jnp.dot(
            weights.reshape(frame_count * row_count, lanes),
            spread,
            preferred_element_type=jnp.float32,
        ).reshape(frame_count, row_count, model_width)
        out_ref[frame] = jnp.sum(wide * v_ref[...].astype(jnp.float32), axis=0).astype(
            jnp.bfloat16
        )
        return carry

    lax.fori_loop(0, frame_count, one_frame, 0)


def time_attention(queries, key_rows, value_rows, clip_lengths):
    frame_count, place_count, model_width = queries.shape
    head_size = model_width // HEADS
    lanes = -(-HEADS // 128) * 128
    row_block = math.gcd(place_count, 16)
    fold = (
        jnp.arange(model_width, dtype=jnp.int32)[:, None] // head_size
        == jnp.arange(lanes, dtype=jnp.int32)[None, :]
    ).astype(jnp.bfloat16)
    block = pl.BlockSpec((frame_count, row_block, model_width), lambda i: (0, i, 0))
    return pl.pallas_call(
        functools.partial(time_kernel, head_size),
        grid=(place_count // row_block,),
        out_shape=jax.ShapeDtypeStruct(queries.shape, jnp.bfloat16),
        in_specs=[
            pl.BlockSpec(memory_space=pltpu.SMEM),
            block,
            block,
            block,
            pl.BlockSpec((model_width, lanes), lambda i: (0, 0)),
            pl.BlockSpec((lanes, model_width), lambda i: (0, 0)),
        ],
        out_specs=block,
        cost_estimate=pl.CostEstimate(
            flops=6 * frame_count * queries.size * lanes,
            bytes_accessed=8 * queries.size,
            transcendentals=0,
        ),
    )(clip_lengths, queries, key_rows, value_rows, fold, fold.T)


def space_attention(projected):
    clip_count, place_count, triple = projected.shape
    model_width = triple // 3
    head_size = model_width // HEADS
    split_parts = projected.reshape(clip_count, place_count, 3, HEADS, head_size)
    scores = jnp.einsum(
        "cphd,cqhd->chpq",
        split_parts[:, :, 0],
        split_parts[:, :, 1],
        preferred_element_type=jnp.float32,
    ) / math.sqrt(head_size)
    weights = softmax_rows(scores)
    attended = jnp.einsum(
        "chpq,cqhd->cphd", weights, split_parts[:, :, 2], preferred_element_type=jnp.float32
    )
    return attended.astype(jnp.bfloat16).reshape(clip_count, place_count, model_width)


def expert_slots(routes):
    onehot = (routes[..., None] == jnp.arange(EXPERTS, dtype=jnp.int32)).astype(jnp.int32)
    earlier = jnp.cumsum(onehot, axis=-2) - onehot
    return jnp.sum(earlier * onehot, axis=-1)


def shards(
    patches,
    temporal_q,
    temporal_k,
    temporal_v,
    clip_lengths,
    w_time,
    gain_space,
    w_space,
    w_merge,
    gain_mix,
    expert_ids,
    gate_weights,
    w_expand,
    w_reduce,
):
    local_shape = patches.shape
    model_width = local_shape[-1]
    frame_size = lax.axis_size("frame")

    def by_place(array_in):
        return lax.all_to_all(
            array_in.reshape(frame_size, -1, model_width),
            "frame",
            split_axis=0,
            concat_axis=0,
            tiled=True,
        )

    tube_out = time_attention(
        by_place(temporal_q), by_place(temporal_k), by_place(temporal_v), clip_lengths
    )
    time_mixed = lax.all_to_all(tube_out, "frame", split_axis=0, concat_axis=0, tiled=True)
    after_time = patches.astype(jnp.float32) + jnp.dot(
        time_mixed.reshape(-1, model_width), w_time, preferred_element_type=jnp.float32
    ).reshape(local_shape)
    normed = layer_norm(after_time, gain_space).reshape(-1, model_width)
    projected = jnp.dot(
        normed,
        lax.all_gather(w_space, "frame", axis=1, tiled=True),
        preferred_element_type=jnp.float32,
    ).astype(jnp.bfloat16)
    projected = projected.reshape(local_shape[0], local_shape[1], local_shape[2], 3 * model_width)
    spatial = lax.map(space_attention, projected)
    after_space = after_time + jnp.dot(
        spatial.reshape(-1, model_width), w_merge, preferred_element_type=jnp.float32
    ).reshape(local_shape)
    mixed_in = layer_norm(after_space, gain_mix).reshape(-1, model_width)
    row_count = mixed_in.shape[0]
    capacity = CAP
    routes = expert_ids.reshape(1, row_count * 2)
    slot_index = expert_slots(routes)[0]
    route_pairs = routes[0].reshape(row_count, 2)
    slot_pairs = slot_index.reshape(row_count, 2)
    expert_size = lax.axis_size("expert")
    shard_count = frame_size * expert_size // EXPERTS
    expand_block = w_expand[0]
    reduce_block = w_reduce[0]
    gate_rows = gate_weights.reshape(row_count, 2)

    def places(first, width):
        local = slot_pairs - first
        number = jnp.where(
            (local >= 0) & (local < width), route_pairs * width + local, -1
        )
        return number[:, :, None] == jnp.arange(EXPERTS * width, dtype=jnp.int32)

    def exchange(array_in):
        return lax.all_to_all(
            array_in, ("frame", "expert"), split_axis=0, concat_axis=0, tiled=True
        )

    def outgoing_rows(hits):
        chosen = jnp.any(hits, axis=1).astype(jnp.bfloat16)
        return jnp.einsum("re,rd->ed", chosen, mixed_in, preferred_element_type=jnp.float32).astype(
            jnp.bfloat16
        )

    def send(rows, width):
        outgoing = rows.reshape((EXPERTS,) + slot_shape(width))
        return exchange(jnp.repeat(outgoing, shard_count, axis=0))

    def slot_shape(width):
        split = 8 // math.gcd(width, 8)
        return (width * split, model_width // split)

    def run_expert(rows):
        hidden = jax.nn.gelu(
            jnp.dot(rows, expand_block, preferred_element_type=jnp.float32), approximate=False
        ).astype(jnp.bfloat16)
        return jnp.dot(hidden, reduce_block, preferred_element_type=jnp.float32).astype(
            jnp.bfloat16
        )

    def mixed_rows(hits, returned, width):
        table = returned.reshape(EXPERTS, shard_count, width * model_width)
        gates = jnp.sum(jnp.where(hits, gate_rows[:, :, None], 0.0), axis=1)
        total = jnp.zeros((row_count, model_width), jnp.float32)
        upper = gates.astype(jnp.bfloat16)
        lower = (gates - upper.astype(jnp.float32)).astype(jnp.bfloat16)
        for shard in range(shard_count):
            block = table[:, shard].reshape(EXPERTS * width, model_width)
            total = total + jnp.dot(upper, block, preferred_element_type=jnp.float32)
            total = total + jnp.dot(lower, block, preferred_element_type=jnp.float32)
        return total

    first_width = capacity // 16 * 8
    widths = (first_width, capacity - first_width)
    hits = (places(0, widths[0]), places(widths[0], widths[1]))
    device_count = EXPERTS * shard_count
    leaving = [outgoing_rows(hit) for hit in hits]
    with jax.named_scope("send_first"):
        first = send(leaving[0], widths[0])
    first, later = lax.optimization_barrier((first, leaving[1]))
    with jax.named_scope("send_second"):
        second = send(later, widths[1])
    with jax.named_scope("expert_first"):
        first_result = run_expert(first.reshape(-1, model_width))
    second, first_result = lax.optimization_barrier((second, first_result))
    with jax.named_scope("back_first"):
        first_back = exchange(first_result.reshape((device_count,) + slot_shape(widths[0])))
    with jax.named_scope("expert_second"):
        second_result = run_expert(second.reshape(-1, model_width))
    with jax.named_scope("back_second"):
        second_back = exchange(second_result.reshape((device_count,) + slot_shape(widths[1])))
    expert_mix = mixed_rows(hits[0], first_back, widths[0])
    expert_mix = expert_mix + mixed_rows(hits[1], second_back, widths[1])
    return (after_space + expert_mix.reshape(local_shape)).astype(jnp.bfloat16)


def solution(mesh):
    return jax.shard_map(
        shards,
        mesh=mesh,
        in_specs=(
            P("frame", "expert", None, None),
            P("frame", "expert", None, None),
            P("frame", "expert", None, None),
            P("frame", "expert", None, None),
            P("expert"),
            P(),
            P(),
            P(None, "frame"),
            P(),
            P(),
            P("frame", "expert", None, None),
            P("frame", "expert", None, None),
            P(("frame", "expert"), None, None),
            P(("frame", "expert"), None, None),
        ),
        out_specs=P("frame", "expert", None, None),
        check_vma=False,
    )
```
